32 devices in a mesh: row: 8 (over y, x, core), col: 4 (over z).
Axes of the slice: x: 2, y: 2, z: 4, core: 2. Of those that a mesh axis runs over, the one named last changes fastest.
Arguments:
- matrix: float32 [5120, 5120], P('row', 'col'), may hold values from -64 to 64
Outputs:
- iterate: float32 [5120, 5120], P('row', 'col')
- trace_value: float32 [2], replicated
- frobenius: float32 [2], replicated
The draws below stay inside these ranges and needn't reach their ends.
All inputs are finite; a program needn't handle non-finite values.
Results may differ from the reference program's by a relative error of at most 0.003.
Values may be sent and summed in bfloat16 or wider, within the bound.
A program may use at most 64 MiB of HBM per device.

```python
import math
import jax
import jax.numpy as jnp

ORDER = 5120


def draw_matrix(key, part):
    first, second, third = jax.random.split(key, 3)
    ramp = jnp.arange(ORDER, dtype=jnp.float32) / max(ORDER - 1, 1)
    raw = jax.random.truncated_normal(first, -5.0, 5.0, (ORDER, ORDER), jnp.float32)
    base = jnp.exp(jax.random.uniform(second, (ORDER,), jnp.float32, math.log(0.6), math.log(1.9)))
    shift = jax.random.uniform(third, (ORDER,), jnp.float32, -0.5, 1.5)
    scales = base * (1.0 + 0.7 * ramp)
    wigner = (raw + raw.T) / jnp.sqrt(2.0 * ORDER)
    inner = wigner + jnp.diag(shift)
    return scales[:, None] * inner * scales[None, :]


def setup_inputs(seed: int = 0) -> dict:
    splits = jax.random.split(jax.random.key(seed), 2)
    matrix = draw_matrix(jax.random.fold_in(splits[1], 71), 0)
    return dict(matrix=matrix)


target = 0.0625

def sign_step(current, rounded, scale, root):
    product = jnp.dot(rounded, rounded, preferred_element_type=jnp.float32)
    squared = (product * scale).astype(jnp.bfloat16)
    cubic_part = jnp.dot(squared, rounded, preferred_element_type=jnp.float32)
    return root * (1.5 * current - 0.5 * cubic_part)

def reference(matrix):
    rounded = matrix.astype(jnp.bfloat16)
    widened = rounded.astype(jnp.float32)
    squares = jnp.sum(widened * widened)
    factor = target * ORDER / (squares + 1e-06)
    first = sign_step(widened, rounded, factor, jnp.sqrt(factor))
    second = sign_step(first, first.astype(jnp.bfloat16), jnp.float32(1.0), jnp.float32(1.0))
    traces = jnp.stack([jnp.sum(jnp.diagonal(first)), jnp.sum(jnp.diagonal(second))])
    norms = jnp.stack([jnp.sqrt(jnp.sum(first * first)), jnp.sqrt(jnp.sum(second * second))])
    return (second, traces, norms)
```

```python
import functools

import jax
import jax.numpy as jnp
from jax import lax
from jax.experimental import pallas as pl
from jax.experimental.pallas import tpu as pltpu
from jax.sharding import PartitionSpec as P

ITERS = 2
TILE = 256
MESH = pl.DeviceIdType.MESH

target = 0.0625


def add_columns(portion, left_panel):
    return jnp.dot(left_panel, portion, preferred_element_type=jnp.float32)


def on_device(matrix):
    rounded = matrix.astype(jnp.bfloat16)
    current = rounded.astype(jnp.float32)
    row_ids = lax.axis_index("row") * matrix.shape[0] + lax.broadcasted_iota(
        jnp.int32, matrix.shape, 0
    )
    col_ids = lax.axis_index("col") * matrix.shape[1] + lax.broadcasted_iota(
        jnp.int32, matrix.shape, 1
    )
    on_diagonal = row_ids == col_ids
    traces = []
    norms = []
    for step in range(ITERS):
        row_panel = lax.all_gather(rounded, "col", axis=1, tiled=True)
        if step == 0:
            order_full = row_panel.shape[1]
            squares = lax.psum(jnp.sum(current * current), ("row", "col"))
            scale = target * order_full / (squares + 1e-06)
            root = jnp.sqrt(scale)
        else:
            scale = jnp.float32(1.0)
            root = jnp.float32(1.0)
        product = add_columns(
            lax.all_gather(rounded, "row", axis=0, tiled=True), left_panel=row_panel
        )
        squared = (product * scale).astype(jnp.bfloat16)
        cubic_part = add_columns(
            lax.all_gather(squared, "row", axis=0, tiled=True), left_panel=row_panel
        )
        current = root * (1.5 * current - 0.5 * cubic_part)
        rounded = current.astype(jnp.bfloat16)
        diagonal_part = jnp.sum(jnp.where(on_diagonal, current, 0.0))
        square_part = jnp.sum(current * current)
        trace_now, total_now = lax.psum((diagonal_part, square_part), ("row", "col"))
        traces.append(trace_now)
        norms.append(jnp.sqrt(total_now))
    return (current, jnp.stack(traces), jnp.stack(norms))


FROM_X, FROM_Y, FROM_SIB, SIB_X, SIB_Y, FROM_D, SIB_D = range(7)
KINDS = 7


def kernel(
    n_row,
    n_col,
    matrix_ref,
    out_ref,
    trace_ref,
    frob_ref,
    panel1,
    panel2,
    cols,
    squares,
    current,
    stats,
    slots_row,
    slots_col,
    xy_send,
    xy_recv,
    z_send,
    z_recv,
    red_send,
    red_recv,
    load_sem,
    store_sem,
):
    rows, width = matrix_ref.shape
    tiles = width // TILE
    half = rows // 2
    order = rows * n_row
    r = lax.axis_index("row")
    z = lax.axis_index("col")
    core = lax.rem(r, 2)
    x = lax.rem(r // 2, 2)
    y = r // 4
    to_sib = 1 - 2 * core
    rs = r + to_sib
    rx = r + 2 - 4 * x
    ry = r + 4 - 8 * y
    rd = rx + 4 - 8 * y
    relay_from = ry * (1 - core) + rx * core
    relay_to = rx * (1 - core) + ry * core
    up = lax.rem(z + 1, n_col)
    down = lax.rem(z + n_col - 1, n_col)
    opposite = lax.rem(z + 2, n_col)

    def load(t):
        return pltpu.make_async_copy(
            matrix_ref.at[:, pl.ds(t * TILE, TILE)], current.at[t], load_sem.at[t]
        )

    def store(t):
        return pltpu.make_async_copy(
            current.at[t],
            out_ref.at[:, pl.ds(pl.multiple_of(t * TILE, TILE), TILE)],
            store_sem.at[t],
        )

    for t in range(tiles):
        load(t).start()

    barrier = pltpu.get_barrier_semaphore()
    for j in range(1, n_row):
        pl.semaphore_signal(
            barrier, inc=1, device_id={"row": lax.rem(r + j, n_row)}, device_id_type=MESH
        )
    for j in range(1, n_col):
        pl.semaphore_signal(
            barrier, inc=1, device_id={"col": lax.rem(z + j, n_col)}, device_id_type=MESH
        )
    pl.semaphore_wait(barrier, n_row + n_col - 2)

    def rows_of(slot):
        return pl.ds(pl.multiple_of(slot * rows, rows), rows)

    def columns_of(slot, t):
        return pl.ds(pl.multiple_of(slot * width + t * TILE, TILE), TILE)

    def xy(buf, phase, t, slot, kind, peer):
        part = buf.at[t, rows_of(slot), :]
        return pltpu.make_async_remote_copy(
            src_ref=part,
            dst_ref=part,
            send_sem=xy_send.at[phase, t, kind],
            recv_sem=xy_recv.at[phase, t, kind],
            device_id={"row": peer},
            device_id_type=MESH,
        )

    def xy_start(buf, phase, t):
        xy(buf, phase, t, r, FROM_X, rx).start()
        xy(buf, phase, t, r, FROM_Y, ry).start()
        xy(buf, phase, t, r, FROM_SIB, rs).start()

    def xy_mid(buf, phase, t):
        xy(buf, phase, t, rx, FROM_X, rx).wait_recv()
        xy(buf, phase, t, ry, FROM_Y, ry).wait_recv()
        xy(buf, phase, t, relay_from, FROM_D, relay_to).start()
        xy(buf, phase, t, rx, SIB_X, rs).start()
        xy(buf, phase, t, ry, SIB_Y, rs).start()

    def xy_fin(buf, phase, t):
        xy(buf, phase, t, rd, FROM_D, rd).wait_recv()
        xy(buf, phase, t, rd, SIB_D, rs).start()

    def xy_done(buf, phase, t):
        xy(buf, phase, t, rs, FROM_SIB, rs).wait_recv()
        xy(buf, phase, t, rx + to_sib, SIB_X, rs).wait_recv()
        xy(buf, phase, t, ry + to_sib, SIB_Y, rs).wait_recv()
        xy(buf, phase, t, rd + to_sib, SIB_D, rs).wait_recv()

    def xy_sent(buf, phase, t):
        xy(buf, phase, t, r, FROM_X, rx).wait_send()
        xy(buf, phase, t, r, FROM_Y, ry).wait_send()
        xy(buf, phase, t, r, FROM_SIB, rs).wait_send()
        xy(buf, phase, t, rx, SIB_X, rs).wait_send()
        xy(buf, phase, t, ry, SIB_Y, rs).wait_send()
        xy(buf, phase, t, relay_from, FROM_D, relay_to).wait_send()
        xy(buf, phase, t, rd, SIB_D, rs).wait_send()

    def zc(panel, step, t, slot, kind, peer):
        if kind < 2:
            part = panel.at[:, columns_of(slot, t)]
        else:
            part = panel.at[pl.ds((kind - 2) * half, half), columns_of(slot, t)]
        return pltpu.make_async_remote_copy(
            src_ref=part,
            dst_ref=part,
            send_sem=z_send.at[step, t, kind],
            recv_sem=z_recv.at[step, t, kind],
            device_id={"col": peer},
            device_id_type=MESH,
        )

    def z_start(panel, step, t):
        zc(panel, step, t, z, 0, up).start()
        zc(panel, step, t, z, 1, down).start()

    def z_mid(panel, step, t):
        zc(panel, step, t, down, 0, up).wait_recv()
        zc(panel, step, t, down, 2, up).start()
        zc(panel, step, t, up, 1, down).wait_recv()
        zc(panel, step, t, up, 3, down).start()

    def z_fin(panel, step, t):
        zc(panel, step, t, opposite, 2, up).wait_recv()
        zc(panel, step, t, opposite, 3, down).wait_recv()

    def z_sent(panel, step, t):
        zc(panel, step, t, z, 0, up).wait_send()
        zc(panel, step, t, z, 1, down).wait_send()
        zc(panel, step, t, down, 2, up).wait_send()
        zc(panel, step, t, up, 3, down).wait_send()

    def red_row(which, j, slot, peer):
        part = slots_row.at[which, slot]
        return pltpu.make_async_remote_copy(
            src_ref=part,
            dst_ref=part,
            send_sem=red_send.at[which, j],
            recv_sem=red_recv.at[which, j],
            device_id={"row": peer},
            device_id_type=MESH,
        )

    def red_col(which, j, slot, peer):
        part = slots_col.at[which, slot]
        return pltpu.make_async_remote_copy(
            src_ref=part,
            dst_ref=part,
            send_sem=red_send.at[which, n_row + j],
            recv_sem=red_recv.at[which, n_row + j],
            device_id={"col": peer},
            device_id_type=MESH,
        )

    def reduce_start(which, value):
        slots_row[which, r] = value
        for j in range(1, n_row):
            red_row(which, j, r, lax.rem(r + j, n_row)).start()

    def reduce_mid(which):
        for j in range(1, n_row):
            back = lax.rem(r + n_row - j, n_row)
            red_row(which, j, back, back).wait_recv()
        total = slots_row[which, 0]
        for s in range(1, n_row):
            total = total + slots_row[which, s]
        slots_col[which, z] = total
        for j in range(1, n_col):
            red_col(which, j, z, lax.rem(z + j, n_col)).start()

    def reduce_end(which):
        for j in range(1, n_col):
            back = lax.rem(z + n_col - j, n_col)
            red_col(which, j, back, back).wait_recv()
        total = slots_col[which, 0]
        for s in range(1, n_col):
            total = total + slots_col[which, s]
        for j in range(1, n_row):
            red_row(which, j, r, lax.rem(r + j, n_row)).wait_send()
        for j in range(1, n_col):
            red_col(which, j, z, lax.rem(z + j, n_col)).wait_send()
        return total

    def lanes(v):
        s = jnp.sum(v, axis=0, keepdims=True)
        out = s[:, 0:128]
        for i in range(1, TILE // 128):
            out = out + s[:, i * 128 : (i + 1) * 128]
        return out

    def add_stats(k, t, v):
        row_ids = r * rows + lax.broadcasted_iota(jnp.int32, v.shape, 0)
        col_ids = z * width + t * TILE + lax.broadcasted_iota(jnp.int32, v.shape, 1)
        stats[k : k + 1, :] += lanes(jnp.where(row_ids == col_ids, v, 0.0))
        stats[k + 1 : k + 2, :] += lanes(v * v)

    stats[...] = jnp.zeros_like(stats)
    for t in range(tiles):
        load(t).wait()
        rounded = current[t].astype(jnp.bfloat16)
        panel1[:, columns_of(z, t)] = rounded
        cols[t, rows_of(r), :] = rounded
        xy_start(cols, 0, t)
        z_start(panel1, 0, t)
        wide = rounded.astype(jnp.float32)
        stats[4:5, :] += lanes(wide * wide)
    reduce_start(0, stats[...])
    reduce_mid(0)

    def product_phase(step, panel, scale):
        phase = 2 * step

        def mid(t, carry):
            xy_mid(cols, phase, t)
            z_mid(panel, step, t)
            return carry

        lax.fori_loop(0, tiles, mid, 0)

        def fin(t, carry):
            z_fin(panel, step, t)
            return carry

        lax.fori_loop(0, tiles, fin, 0)
        xy_fin(cols, phase, 0)

        def work(t, carry):
            @pl.when(t < tiles - 1)
            def _():
                xy_fin(cols, phase, t + 1)

            xy_done(cols, phase, t)
            product = jnp.dot(panel[...], cols[t], preferred_element_type=jnp.float32)
            if scale is not None:
                product = product * scale
            squares[t, rows_of(r), :] = product.astype(jnp.bfloat16)
            xy_sent(cols, phase, t)
            xy_start(squares, phase + 1, t)
            return carry

        lax.fori_loop(0, tiles, work, 0)

    def cubic_phase(step, panel, finish):
        phase = 2 * step + 1

        def mid(t, carry):
            xy_mid(squares, phase, t)
            return carry

        lax.fori_loop(0, tiles, mid, 0)
        xy_fin(squares, phase, 0)

        def work(t, carry):
            @pl.when(t < tiles - 1)
            def _():
                xy_fin(squares, phase, t + 1)

            xy_done(squares, phase, t)
            cubic = jnp.dot(panel[...], squares[t], preferred_element_type=jnp.float32)
            xy_sent(squares, phase, t)
            finish(t, cubic)
            return carry

        lax.fori_loop(0, tiles, work, 0)

    total = reduce_end(0)
    scale = target * order / (jnp.sum(total[4:5, :], axis=1, keepdims=True) + 1e-06)
    root = jnp.sqrt(scale)

    product_phase(0, panel1, scale)

    def finish_first(t, cubic):
        wide = panel1[:, columns_of(z, t)].astype(jnp.float32)
        value = root * (1.5 * wide - 0.5 * cubic)
        current[t] = value
        rounded = value.astype(jnp.bfloat16)
        panel2[:, columns_of(z, t)] = rounded
        cols[t, rows_of(r), :] = rounded
        xy_start(cols, 2, t)
        z_start(panel2, 1, t)
        add_stats(0, t, value)

    cubic_phase(0, panel1, finish_first)
    product_phase(1, panel2, None)

    def finish_second(t, cubic):
        value = 1.5 * current[t] - 0.5 * cubic
        current[t] = value
        store(t).start()
        add_stats(2, t, value)

    cubic_phase(1, panel2, finish_second)

    reduce_start(1, stats[...])
    reduce_mid(1)
    total = reduce_end(1)
    sums = jnp.sum(total, axis=1, keepdims=True)
    norms = jnp.sqrt(sums)
    trace_ref[0] = sums[0, 0]
    trace_ref[1] = sums[2, 0]
    frob_ref[0] = norms[1, 0]
    frob_ref[1] = norms[3, 0]

    def clear(t, carry):
        z_sent(panel1, 0, t)
        z_sent(panel2, 1, t)
        store(t).wait()
        return carry

    lax.fori_loop(0, tiles, clear, 0)


def in_one_kernel(n_row, n_col, matrix):
    rows, width = matrix.shape
    tiles = width // TILE
    order = rows * n_row
    narrow = jnp.bfloat16
    return pl.pallas_call(
        functools.partial(kernel, n_row, n_col),
        out_shape=(
            jax.ShapeDtypeStruct((rows, width), jnp.float32),
            jax.ShapeDtypeStruct((ITERS,), jnp.float32),
            jax.ShapeDtypeStruct((ITERS,), jnp.float32),
        ),
        in_specs=[pl.BlockSpec(memory_space=pl.ANY)],
        out_specs=(
            pl.BlockSpec(memory_space=pl.ANY),
            pl.BlockSpec(memory_space=pltpu.SMEM),
            pl.BlockSpec(memory_space=pltpu.SMEM),
        ),
        scratch_shapes=[
            pltpu.VMEM((rows, width * n_col), narrow),
            pltpu.VMEM((rows, width * n_col), narrow),
            pltpu.VMEM((tiles, order, TILE), narrow),
            pltpu.VMEM((tiles, order, TILE), narrow),
            pltpu.VMEM((tiles, rows, TILE), jnp.float32),
            pltpu.VMEM((8, 128), jnp.float32),
            pltpu.VMEM((2, n_row, 8, 128), jnp.float32),
            pltpu.VMEM((2, n_col, 8, 128), jnp.float32),
            pltpu.SemaphoreType.DMA((2 * ITERS, tiles, KINDS)),
            pltpu.SemaphoreType.DMA((2 * ITERS, tiles, KINDS)),
            pltpu.SemaphoreType.DMA((ITERS, tiles, 4)),
            pltpu.SemaphoreType.DMA((ITERS, tiles, 4)),
            pltpu.SemaphoreType.DMA((2, n_row + n_col)),
            pltpu.SemaphoreType.DMA((2, n_row + n_col)),
            pltpu.SemaphoreType.DMA((tiles,)),
            pltpu.SemaphoreType.DMA((tiles,)),
        ],
        compiler_params=pltpu.CompilerParams(
            collective_id=0, has_side_effects=True, vmem_limit_bytes=60 * 1024 * 1024
        ),
    )(matrix)


def solution(mesh):
    in_specs = (P("row", "col"),)
    out_specs = (P("row", "col"), P(), P())
    n_row, n_col = mesh.shape["row"], mesh.shape["col"]

    def body(matrix):
        square_plane = n_row == 2 * 2 * 2 and n_col == 2 * 2
        if square_plane and matrix.shape[1] % TILE == 0 and matrix.shape[0] % 32 == 0:
            return in_one_kernel(n_row, n_col, matrix)
        return on_device(matrix)

    return jax.shard_map(
        body, mesh=mesh, in_specs=in_specs, out_specs=out_specs, check_vma=False
    )
```

```python
import functools

import jax
import jax.numpy as jnp
from jax import lax
from jax.experimental import pallas as pl
from jax.experimental.pallas import tpu as pltpu
from jax.sharding import PartitionSpec as P

ITERS = 2
TILE = 256
MESH = pl.DeviceIdType.MESH

target = 0.0625


def add_columns(portion, left_panel):
    return jnp.dot(left_panel, portion, preferred_element_type=jnp.float32)


def on_device(matrix):
    rounded = matrix.astype(jnp.bfloat16)
    current = rounded.astype(jnp.float32)
    row_ids = lax.axis_index("row") * matrix.shape[0] + lax.broadcasted_iota(
        jnp.int32, matrix.shape, 0
    )
    col_ids = lax.axis_index("col") * matrix.shape[1] + lax.broadcasted_iota(
        jnp.int32, matrix.shape, 1
    )
    on_diagonal = row_ids == col_ids
    traces = []
    norms = []
    for step in range(ITERS):
        row_panel = lax.all_gather(rounded, "col", axis=1, tiled=True)
        if step == 0:
            order_full = row_panel.shape[1]
            squares = lax.psum(jnp.sum(current * current), ("row", "col"))
            scale = target * order_full / (squares + 1e-06)
            root = jnp.sqrt(scale)
        else:
            scale = jnp.float32(1.0)
            root = jnp.float32(1.0)
        product = add_columns(
            lax.all_gather(rounded, "row", axis=0, tiled=True), left_panel=row_panel
        )
        squared = (product * scale).astype(jnp.bfloat16)
        cubic_part = add_columns(
            lax.all_gather(squared, "row", axis=0, tiled=True), left_panel=row_panel
        )
        current = root * (1.5 * current - 0.5 * cubic_part)
        rounded = current.astype(jnp.bfloat16)
        diagonal_part = jnp.sum(jnp.where(on_diagonal, current, 0.0))
        square_part = jnp.sum(current * current)
        trace_now, total_now = lax.psum((diagonal_part, square_part), ("row", "col"))
        traces.append(trace_now)
        norms.append(jnp.sqrt(total_now))
    return (current, jnp.stack(traces), jnp.stack(norms))


FROM_X, FROM_Y, FROM_SIB, SIB_X, SIB_Y, FROM_D, SIB_D = range(7)
KINDS = 7
LAG = 2


def row_parts(rows):
    fifth = rows // 5
    return ((0, 2 * fifth), (2 * fifth, 2 * fifth), (4 * fifth, fifth))


def kernel(
    n_row,
    n_col,
    matrix_ref,
    out_ref,
    trace_ref,
    frob_ref,
    panel1,
    panel2,
    cols,
    squares,
    current,
    stats,
    slots_row,
    slots_col,
    xy_send,
    xy_recv,
    z_send,
    z_recv,
    red_send,
    red_recv,
    load_sem,
    store_sem,
):
    rows, width = matrix_ref.shape
    tiles = width // TILE
    order = rows * n_row
    panels = (panel1, panel2)
    parts = row_parts(rows)
    n_parts = len(parts)
    r = lax.axis_index("row")
    z = lax.axis_index("col")
    core = lax.rem(r, 2)
    x = lax.rem(r // 2, 2)
    y = r // 4
    to_sib = 1 - 2 * core
    rs = r + to_sib
    rx = r + 2 - 4 * x
    ry = r + 4 - 8 * y
    rd = rx + 4 - 8 * y
    relay_from = ry * (1 - core) + rx * core
    relay_to = rx * (1 - core) + ry * core
    up = lax.rem(z + 1, n_col)
    down = lax.rem(z + n_col - 1, n_col)

    def load(t):
        return pltpu.make_async_copy(
            matrix_ref.at[:, pl.ds(t * TILE, TILE)], current.at[t], load_sem.at[t]
        )

    def store(t):
        return pltpu.make_async_copy(
            current.at[t],
            out_ref.at[:, pl.ds(pl.multiple_of(t * TILE, TILE), TILE)],
            store_sem.at[t],
        )

    for t in range(tiles):
        load(t).start()

    barrier = pltpu.get_barrier_semaphore()
    for j in range(1, n_row):
        pl.semaphore_signal(
            barrier, inc=1, device_id={"row": lax.rem(r + j, n_row)}, device_id_type=MESH
        )
    for j in range(1, n_col):
        pl.semaphore_signal(
            barrier, inc=1, device_id={"col": lax.rem(z + j, n_col)}, device_id_type=MESH
        )
    pl.semaphore_wait(barrier, n_row + n_col - 2)

    def rows_of(slot, part=None):
        offset, size = (0, rows) if part is None else parts[part]
        return pl.ds(pl.multiple_of(slot * rows + offset, 16), size)

    def columns_of(slot, t):
        return pl.ds(pl.multiple_of(slot * width + t * TILE, TILE), TILE)

    def xy(buf, step, part, t, slot, kind, peer):
        block = buf.at[t, rows_of(slot, part), :]
        phase = step * (n_parts + 1) + (0 if part is None else part + 1)
        return pltpu.make_async_remote_copy(
            src_ref=block,
            dst_ref=block,
            send_sem=xy_send.at[phase, t, kind],
            recv_sem=xy_recv.at[phase, t, kind],
            device_id={"row": peer},
            device_id_type=MESH,
        )

    def xy_start(*to):
        xy(*to, r, FROM_X, rx).start()
        xy(*to, r, FROM_Y, ry).start()
        xy(*to, r, FROM_SIB, rs).start()

    def xy_mid(*to):
        xy(*to, rx, FROM_X, rx).wait_recv()
        xy(*to, ry, FROM_Y, ry).wait_recv()
        xy(*to, relay_from, FROM_D, relay_to).start()
        xy(*to, rx, SIB_X, rs).start()
        xy(*to, ry, SIB_Y, rs).start()

    def xy_fin(*to):
        xy(*to, rd, FROM_D, rd).wait_recv()
        xy(*to, rd, SIB_D, rs).start()

    def xy_done(*to):
        xy(*to, rs, FROM_SIB, rs).wait_recv()
        xy(*to, rx + to_sib, SIB_X, rs).wait_recv()
        xy(*to, ry + to_sib, SIB_Y, rs).wait_recv()
        xy(*to, rd + to_sib, SIB_D, rs).wait_recv()

    def xy_sent(*to):
        xy(*to, r, FROM_X, rx).wait_send()
        xy(*to, r, FROM_Y, ry).wait_send()
        xy(*to, r, FROM_SIB, rs).wait_send()
        xy(*to, rx, SIB_X, rs).wait_send()
        xy(*to, ry, SIB_Y, rs).wait_send()
        xy(*to, relay_from, FROM_D, relay_to).wait_send()
        xy(*to, rd, SIB_D, rs).wait_send()

    def zc(step, part, t, level, upward, slot, peer):
        offset, size = parts[part]
        block = panels[step].at[pl.ds(offset, size), columns_of(slot, t)]
        kind = 2 * (level - 1) + upward
        phase = step * n_parts + part
        return pltpu.make_async_remote_copy(
            src_ref=block,
            dst_ref=block,
            send_sem=z_send.at[phase, t, kind],
            recv_sem=z_recv.at[phase, t, kind],
            device_id={"col": peer},
            device_id_type=MESH,
        )

    def z_send_level(step, part, t, level, act):
        far = level - 1

        @pl.when((z >= far) & (z < n_col - 1))
        def _():
            act(zc(step, part, t, level, 1, lax.rem(z + n_col - far, n_col), up))

        @pl.when((z < n_col - far) & (z > 0))
        def _():
            act(zc(step, part, t, level, 0, lax.rem(z + far, n_col), down))

    def z_wait_level(step, part, t, level):
        @pl.when(z >= level)
        def _():
            zc(step, part, t, level, 1, lax.rem(z + n_col - level, n_col), up).wait_recv()

        @pl.when(z < n_col - level)
        def _():
            zc(step, part, t, level, 0, lax.rem(z + level, n_col), down).wait_recv()

    def z_start(step, part, t):
        z_send_level(step, part, t, 1, lambda copy: copy.start())

    def z_relay(step, part, t, level):
        z_wait_level(step, part, t, level)
        if level < n_col - 1:
            z_send_level(step, part, t, level + 1, lambda copy: copy.start())

    def z_sent(step, part, t):
        for level in range(1, n_col):
            z_send_level(step, part, t, level, lambda copy: copy.wait_send())

    def over_tiles(work, start=0, stop=None):
        def body(t, carry):
            work(t)
            return carry

        lax.fori_loop(start, tiles if stop is None else stop, body, 0)

    def red_row(which, j, slot, peer):
        part = slots_row.at[which, slot]
        return pltpu.make_async_remote_copy(
            src_ref=part,
            dst_ref=part,
            send_sem=red_send.at[which, j],
            recv_sem=red_recv.at[which, j],
            device_id={"row": peer},
            device_id_type=MESH,
        )

    def red_col(which, j, slot, peer):
        part = slots_col.at[which, slot]
        return pltpu.make_async_remote_copy(
            src_ref=part,
            dst_ref=part,
            send_sem=red_send.at[which, n_row + j],
            recv_sem=red_recv.at[which, n_row + j],
            device_id={"col": peer},
            device_id_type=MESH,
        )

    def reduce_start(which, value):
        slots_row[which, r] = value
        for j in range(1, n_row):
            red_row(which, j, r, lax.rem(r + j, n_row)).start()

    def reduce_mid(which):
        for j in range(1, n_row):
            back = lax.rem(r + n_row - j, n_row)
            red_row(which, j, back, back).wait_recv()
        total = slots_row[which, 0]
        for s in range(1, n_row):
            total = total + slots_row[which, s]
        slots_col[which, z] = total
        for j in range(1, n_col):
            red_col(which, j, z, lax.rem(z + j, n_col)).start()

    def reduce_end(which):
        for j in range(1, n_col):
            back = lax.rem(z + n_col - j, n_col)
            red_col(which, j, back, back).wait_recv()
        total = slots_col[which, 0]
        for s in range(1, n_col):
            total = total + slots_col[which, s]
        for j in range(1, n_row):
            red_row(which, j, r, lax.rem(r + j, n_row)).wait_send()
        for j in range(1, n_col):
            red_col(which, j, z, lax.rem(z + j, n_col)).wait_send()
        return total

    def lanes(v):
        s = jnp.sum(v, axis=0, keepdims=True)
        out = s[:, 0:128]
        for i in range(1, TILE // 128):
            out = out + s[:, i * 128 : (i + 1) * 128]
        return out

    def add_stats(k, t, v):
        row_ids = r * rows + lax.broadcasted_iota(jnp.int32, v.shape, 0)
        col_ids = z * width + t * TILE + lax.broadcasted_iota(jnp.int32, v.shape, 1)
        stats[k : k + 1, :] += lanes(jnp.where(row_ids == col_ids, v, 0.0))
        stats[k + 1 : k + 2, :] += lanes(v * v)

    stats[...] = jnp.zeros_like(stats)
    for t in range(tiles):
        load(t).wait()
        rounded = current[t].astype(jnp.bfloat16)
        panel1[:, columns_of(z, t)] = rounded
        cols[t, rows_of(r), :] = rounded
        z_start(0, 0, t)
        xy_start(cols, 0, None, t)
        wide = rounded.astype(jnp.float32)
        stats[4:5, :] += lanes(wide * wide)
    reduce_start(0, stats[...])

    def step_of(step, scale_now, finish):
        panel = panels[step]
        last = n_parts - 1

        def first_pass(t):
            z_relay(step, 0, t, 1)
            xy_mid(cols, step, None, t)

        over_tiles(first_pass)
        for level in range(2, n_col - 1):
            over_tiles(lambda t: z_relay(step, 0, t, level))
        over_tiles(lambda t: z_start(step, 1, t))
        over_tiles(lambda t: xy_fin(cols, step, None, t))
        over_tiles(lambda t: z_relay(step, 0, t, n_col - 1))
        scale = scale_now()

        for part in range(n_parts):
            if part > 0:

                def pass_one(t):
                    z_relay(step, part, t, 1)
                    xy_mid(squares, step, part - 1, t)

                over_tiles(pass_one)
                for level in range(2, n_col - 1):
                    over_tiles(lambda t: z_relay(step, part, t, level))
                if part < last:
                    over_tiles(lambda t: z_start(step, part + 1, t))
                over_tiles(lambda t: xy_fin(squares, step, part - 1, t))
                over_tiles(lambda t: z_relay(step, part, t, n_col - 1))

            def product_tile(t):
                if part == 0:
                    xy_done(cols, step, None, t)
                offset, size = parts[part]
                product = jnp.dot(
                    panel[offset : offset + size, :],
                    cols[t],
                    preferred_element_type=jnp.float32,
                )
                if scale is not None:
                    product = product * scale
                squares[t, rows_of(r, part), :] = product.astype(jnp.bfloat16)
                if part == 0:
                    xy_sent(cols, step, None, t)
                xy_start(squares, step, part, t)
                if part == last:

                    @pl.when(t >= LAG)
                    def _():
                        xy_mid(squares, step, part, t - LAG)

            over_tiles(product_tile)

        over_tiles(lambda t: xy_mid(squares, step, last, t), tiles - LAG)
        xy_fin(squares, step, last, 0)

        def cubic_tile(t):
            @pl.when(t < tiles - 1)
            def _():
                xy_fin(squares, step, last, t + 1)

            for part in range(n_parts):
                xy_done(squares, step, part, t)
            cubic = jnp.dot(panel[...], squares[t], preferred_element_type=jnp.float32)
            for part in range(n_parts):
                xy_sent(squares, step, part, t)
            finish(t, cubic)

        over_tiles(cubic_tile)

    roots = []

    def first_scale():
        reduce_mid(0)
        total = reduce_end(0)
        scale = target * order / (jnp.sum(total[4:5, :], axis=1, keepdims=True) + 1e-06)
        roots.append(jnp.sqrt(scale))
        return scale

    def finish_first(t, cubic):
        wide = panel1[:, columns_of(z, t)].astype(jnp.float32)
        value = roots[0] * (1.5 * wide - 0.5 * cubic)
        current[t] = value
        rounded = value.astype(jnp.bfloat16)
        panel2[:, columns_of(z, t)] = rounded
        cols[t, rows_of(r), :] = rounded
        z_start(1, 0, t)
        xy_start(cols, 1, None, t)
        add_stats(0, t, value)

    def finish_second(t, cubic):
        value = 1.5 * current[t] - 0.5 * cubic
        current[t] = value
        store(t).start()
        add_stats(2, t, value)

    step_of(0, first_scale, finish_first)
    step_of(1, lambda: None, finish_second)

    reduce_start(1, stats[...])
    reduce_mid(1)
    total = reduce_end(1)
    sums = jnp.sum(total, axis=1, keepdims=True)
    norms = jnp.sqrt(sums)
    trace_ref[0] = sums[0, 0]
    trace_ref[1] = sums[2, 0]
    frob_ref[0] = norms[1, 0]
    frob_ref[1] = norms[3, 0]

    def clear(t):
        for step in range(ITERS):
            for part in range(n_parts):
                z_sent(step, part, t)
        store(t).wait()

    over_tiles(clear)


def in_one_kernel(n_row, n_col, matrix):
    rows, width = matrix.shape
    tiles = width // TILE
    order = rows * n_row
    n_parts = len(row_parts(rows))
    narrow = jnp.bfloat16
    return pl.pallas_call(
        functools.partial(kernel, n_row, n_col),
        out_shape=(
            jax.ShapeDtypeStruct((rows, width), jnp.float32),
            jax.ShapeDtypeStruct((ITERS,), jnp.float32),
            jax.ShapeDtypeStruct((ITERS,), jnp.float32),
        ),
        in_specs=[pl.BlockSpec(memory_space=pl.ANY)],
        out_specs=(
            pl.BlockSpec(memory_space=pl.ANY),
            pl.BlockSpec(memory_space=pltpu.SMEM),
            pl.BlockSpec(memory_space=pltpu.SMEM),
        ),
        scratch_shapes=[
            pltpu.VMEM((rows, width * n_col), narrow),
            pltpu.VMEM((rows, width * n_col), narrow),
            pltpu.VMEM((tiles, order, TILE), narrow),
            pltpu.VMEM((tiles, order, TILE), narrow),
            pltpu.VMEM((tiles, rows, TILE), jnp.float32),
            pltpu.VMEM((8, 128), jnp.float32),
            pltpu.VMEM((2, n_row, 8, 128), jnp.float32),
            pltpu.VMEM((2, n_col, 8, 128), jnp.float32),
            pltpu.SemaphoreType.DMA((ITERS * (n_parts + 1), tiles, KINDS)),
            pltpu.SemaphoreType.DMA((ITERS * (n_parts + 1), tiles, KINDS)),
            pltpu.SemaphoreType.DMA((ITERS * n_parts, tiles, 2 * (n_col - 1))),
            pltpu.SemaphoreType.DMA((ITERS * n_parts, tiles, 2 * (n_col - 1))),
            pltpu.SemaphoreType.DMA((2, n_row + n_col)),
            pltpu.SemaphoreType.DMA((2, n_row + n_col)),
            pltpu.SemaphoreType.DMA((tiles,)),
            pltpu.SemaphoreType.DMA((tiles,)),
        ],
        compiler_params=pltpu.CompilerParams(
            collective_id=0, has_side_effects=True, vmem_limit_bytes=60 * 1024 * 1024
        ),
    )(matrix)


def solution(mesh):
    in_specs = (P("row", "col"),)
    out_specs = (P("row", "col"), P(), P())
    n_row, n_col = mesh.shape["row"], mesh.shape["col"]

    def body(matrix):
        square_plane = n_row == 2 * 2 * 2 and n_col == 2 * 2
        if square_plane and matrix.shape[1] % TILE == 0 and matrix.shape[0] % (5 * 16) == 0:
            return in_one_kernel(n_row, n_col, matrix)
        return on_device(matrix)

    return jax.shard_map(
        body, mesh=mesh, in_specs=in_specs, out_specs=out_specs, check_vma=False
    )
```

```python
import functools

import jax
import jax.numpy as jnp
from jax import lax
from jax.experimental import pallas as pl
from jax.experimental.pallas import tpu as pltpu
from jax.sharding import PartitionSpec as P

ITERS = 2
TILE = 256
MESH = pl.DeviceIdType.MESH

target = 0.0625


def add_columns(portion, left_panel):
    return jnp.dot(left_panel, portion, preferred_element_type=jnp.float32)


def on_device(matrix):
    rounded = matrix.astype(jnp.bfloat16)
    current = rounded.astype(jnp.float32)
    row_ids = lax.axis_index("row") * matrix.shape[0] + lax.broadcasted_iota(
        jnp.int32, matrix.shape, 0
    )
    col_ids = lax.axis_index("col") * matrix.shape[1] + lax.broadcasted_iota(
        jnp.int32, matrix.shape, 1
    )
    on_diagonal = row_ids == col_ids
    traces = []
    norms = []
    for step in range(ITERS):
        row_panel = lax.all_gather(rounded, "col", axis=1, tiled=True)
        if step == 0:
            order_full = row_panel.shape[1]
            squares = lax.psum(jnp.sum(current * current), ("row", "col"))
            scale = target * order_full / (squares + 1e-06)
            root = jnp.sqrt(scale)
        else:
            scale = jnp.float32(1.0)
            root = jnp.float32(1.0)
        product = add_columns(
            lax.all_gather(rounded, "row", axis=0, tiled=True), left_panel=row_panel
        )
        squared = (product * scale).astype(jnp.bfloat16)
        cubic_part = add_columns(
            lax.all_gather(squared, "row", axis=0, tiled=True), left_panel=row_panel
        )
        current = root * (1.5 * current - 0.5 * cubic_part)
        rounded = current.astype(jnp.bfloat16)
        diagonal_part = jnp.sum(jnp.where(on_diagonal, current, 0.0))
        square_part = jnp.sum(current * current)
        trace_now, total_now = lax.psum((diagonal_part, square_part), ("row", "col"))
        traces.append(trace_now)
        norms.append(jnp.sqrt(total_now))
    return (current, jnp.stack(traces), jnp.stack(norms))


FROM_X, FROM_Y, FROM_SIB, SIB_X, SIB_Y, FROM_D, SIB_D = range(7)
KINDS = 7
LAG = 2


def row_parts(rows):
    fifth = rows // 5
    return ((0, 2 * fifth), (2 * fifth, 2 * fifth), (4 * fifth, fifth))


def kernel(
    n_row,
    n_col,
    matrix_ref,
    out_ref,
    trace_ref,
    frob_ref,
    panel1,
    panel2,
    cols,
    squares,
    current,
    stats,
    slots_row,
    slots_col,
    xy_send,
    xy_recv,
    z_send,
    z_recv,
    red_send,
    red_recv,
    load_sem,
):
    rows, width = matrix_ref.shape
    tiles = width // TILE
    order = rows * n_row
    panels = (panel1, panel2)
    parts = row_parts(rows)
    n_parts = len(parts)
    r = lax.axis_index("row")
    z = lax.axis_index("col")
    core = lax.rem(r, 2)
    x = lax.rem(r // 2, 2)
    y = r // 4
    to_sib = 1 - 2 * core
    rs = r + to_sib
    rx = r + 2 - 4 * x
    ry = r + 4 - 8 * y
    rd = rx + 4 - 8 * y
    relay_from = ry * (1 - core) + rx * core
    relay_to = rx * (1 - core) + ry * core
    up = lax.rem(z + 1, n_col)
    down = lax.rem(z + n_col - 1, n_col)

    def load(t):
        return pltpu.make_async_copy(
            matrix_ref.at[:, pl.ds(t * TILE, TILE)], current.at[t], load_sem.at[t]
        )

    for t in range(tiles):
        load(t).start()

    barrier = pltpu.get_barrier_semaphore()
    for j in range(1, n_row):
        pl.semaphore_signal(
            barrier, inc=1, device_id={"row": lax.rem(r + j, n_row)}, device_id_type=MESH
        )
    for j in range(1, n_col):
        pl.semaphore_signal(
            barrier, inc=1, device_id={"col": lax.rem(z + j, n_col)}, device_id_type=MESH
        )
    pl.semaphore_wait(barrier, n_row + n_col - 2)

    def rows_of(slot, part=None):
        offset, size = (0, rows) if part is None else parts[part]
        return pl.ds(pl.multiple_of(slot * rows + offset, 16), size)

    def columns_of(slot, t):
        return pl.ds(pl.multiple_of(slot * width + t * TILE, TILE), TILE)

    def xy(buf, step, part, t, slot, kind, peer):
        block = buf.at[t, rows_of(slot, part), :]
        phase = step * (n_parts + 1) + (0 if part is None else part + 1)
        return pltpu.make_async_remote_copy(
            src_ref=block,
            dst_ref=block,
            send_sem=xy_send.at[phase, t, kind],
            recv_sem=xy_recv.at[phase, t, kind],
            device_id={"row": peer},
            device_id_type=MESH,
        )

    def xy_start(*to):
        xy(*to, r, FROM_X, rx).start()
        xy(*to, r, FROM_Y, ry).start()
        xy(*to, r, FROM_SIB, rs).start()

    def xy_mid(*to):
        xy(*to, rx, FROM_X, rx).wait_recv()
        xy(*to, ry, FROM_Y, ry).wait_recv()
        xy(*to, relay_from, FROM_D, relay_to).start()
        xy(*to, rx, SIB_X, rs).start()
        xy(*to, ry, SIB_Y, rs).start()

    def xy_fin(*to):
        xy(*to, rd, FROM_D, rd).wait_recv()
        xy(*to, rd, SIB_D, rs).start()

    def xy_done(*to):
        xy(*to, rs, FROM_SIB, rs).wait_recv()
        xy(*to, rx + to_sib, SIB_X, rs).wait_recv()
        xy(*to, ry + to_sib, SIB_Y, rs).wait_recv()
        xy(*to, rd + to_sib, SIB_D, rs).wait_recv()

    def xy_sent(*to):
        xy(*to, r, FROM_X, rx).wait_send()
        xy(*to, r, FROM_Y, ry).wait_send()
        xy(*to, r, FROM_SIB, rs).wait_send()
        xy(*to, rx, SIB_X, rs).wait_send()
        xy(*to, ry, SIB_Y, rs).wait_send()
        xy(*to, relay_from, FROM_D, relay_to).wait_send()
        xy(*to, rd, SIB_D, rs).wait_send()

    def zc(step, part, t, level, upward, slot, peer):
        offset, size = parts[part]
        block = panels[step].at[pl.ds(offset, size), columns_of(slot, t)]
        kind = 2 * (level - 1) + upward
        phase = step * n_parts + part
        return pltpu.make_async_remote_copy(
            src_ref=block,
            dst_ref=block,
            send_sem=z_send.at[phase, t, kind],
            recv_sem=z_recv.at[phase, t, kind],
            device_id={"col": peer},
            device_id_type=MESH,
        )

    def z_send_level(step, part, t, level, act):
        far = level - 1

        @pl.when((z >= far) & (z < n_col - 1))
        def _():
            act(zc(step, part, t, level, 1, lax.rem(z + n_col - far, n_col), up))

        @pl.when((z < n_col - far) & (z > 0))
        def _():
            act(zc(step, part, t, level, 0, lax.rem(z + far, n_col), down))

    def z_wait_level(step, part, t, level):
        @pl.when(z >= level)
        def _():
            zc(step, part, t, level, 1, lax.rem(z + n_col - level, n_col), up).wait_recv()

        @pl.when(z < n_col - level)
        def _():
            zc(step, part, t, level, 0, lax.rem(z + level, n_col), down).wait_recv()

    def z_start(step, part, t):
        z_send_level(step, part, t, 1, lambda copy: copy.start())

    def z_relay(step, part, t, level):
        z_wait_level(step, part, t, level)
        if level < n_col - 1:
            z_send_level(step, part, t, level + 1, lambda copy: copy.start())

    def z_sent(step, part, t):
        for level in range(1, n_col):
            z_send_level(step, part, t, level, lambda copy: copy.wait_send())

    def over_tiles(work, start=0, stop=None):
        def body(t, carry):
            work(t)
            return carry

        lax.fori_loop(start, tiles if stop is None else stop, body, 0)

    def red_row(which, j, slot, peer):
        part = slots_row.at[which, slot]
        return pltpu.make_async_remote_copy(
            src_ref=part,
            dst_ref=part,
            send_sem=red_send.at[which, j],
            recv_sem=red_recv.at[which, j],
            device_id={"row": peer},
            device_id_type=MESH,
        )

    def red_col(which, j, slot, peer):
        part = slots_col.at[which, slot]
        return pltpu.make_async_remote_copy(
            src_ref=part,
            dst_ref=part,
            send_sem=red_send.at[which, n_row + j],
            recv_sem=red_recv.at[which, n_row + j],
            device_id={"col": peer},
            device_id_type=MESH,
        )

    def reduce_start(which, value):
        slots_row[which, r] = value
        for j in range(1, n_row):
            red_row(which, j, r, lax.rem(r + j, n_row)).start()

    def reduce_mid(which):
        for j in range(1, n_row):
            back = lax.rem(r + n_row - j, n_row)
            red_row(which, j, back, back).wait_recv()
        total = slots_row[which, 0]
        for s in range(1, n_row):
            total = total + slots_row[which, s]
        slots_col[which, z] = total
        for j in range(1, n_col):
            red_col(which, j, z, lax.rem(z + j, n_col)).start()

    def reduce_end(which):
        for j in range(1, n_col):
            back = lax.rem(z + n_col - j, n_col)
            red_col(which, j, back, back).wait_recv()
        total = slots_col[which, 0]
        for s in range(1, n_col):
            total = total + slots_col[which, s]
        for j in range(1, n_row):
            red_row(which, j, r, lax.rem(r + j, n_row)).wait_send()
        for j in range(1, n_col):
            red_col(which, j, z, lax.rem(z + j, n_col)).wait_send()
        return total

    def lanes(v):
        s = jnp.sum(v, axis=0, keepdims=True)
        out = s[:, 0:128]
        for i in range(1, TILE // 128):
            out = out + s[:, i * 128 : (i + 1) * 128]
        return out

    def add_stats(k, t, v):
        row_ids = r * rows + lax.broadcasted_iota(jnp.int32, v.shape, 0)
        col_ids = z * width + t * TILE + lax.broadcasted_iota(jnp.int32, v.shape, 1)
        stats[k : k + 1, :] += lanes(jnp.where(row_ids == col_ids, v, 0.0))
        stats[k + 1 : k + 2, :] += lanes(v * v)

    stats[...] = jnp.zeros_like(stats)
    for t in range(tiles):
        load(t).wait()
        rounded = current[t].astype(jnp.bfloat16)
        panel1[:, columns_of(z, t)] = rounded
        cols[t, rows_of(r), :] = rounded
        z_start(0, 0, t)
        xy_start(cols, 0, None, t)
        wide = rounded.astype(jnp.float32)
        stats[4:5, :] += lanes(wide * wide)
    reduce_start(0, stats[...])

    def step_of(step, scale_now, finish):
        panel = panels[step]
        last = n_parts - 1

        def first_pass(t):
            z_relay(step, 0, t, 1)
            xy_mid(cols, step, None, t)

        over_tiles(first_pass)
        for level in range(2, n_col - 1):
            over_tiles(lambda t: z_relay(step, 0, t, level))
        over_tiles(lambda t: z_start(step, 1, t))
        over_tiles(lambda t: xy_fin(cols, step, None, t))
        over_tiles(lambda t: z_relay(step, 0, t, n_col - 1))
        scale = scale_now()

        for part in range(n_parts):
            if part > 0:

                def pass_one(t):
                    z_relay(step, part, t, 1)
                    xy_mid(squares, step, part - 1, t)

                over_tiles(pass_one)
                for level in range(2, n_col - 1):
                    over_tiles(lambda t: z_relay(step, part, t, level))
                if part < last:
                    over_tiles(lambda t: z_start(step, part + 1, t))
                over_tiles(lambda t: xy_fin(squares, step, part - 1, t))
                over_tiles(lambda t: z_relay(step, part, t, n_col - 1))

            def product_tile(t):
                if part == 0:
                    xy_done(cols, step, None, t)
                offset, size = parts[part]
                product = jnp.dot(
                    panel[offset : offset + size, :],
                    cols[t],
                    preferred_element_type=jnp.float32,
                )
                if scale is not None:
                    product = product * scale
                squares[t, rows_of(r, part), :] = product.astype(jnp.bfloat16)
                if part == 0:
                    xy_sent(cols, step, None, t)
                xy_start(squares, step, part, t)
                if part == last:

                    @pl.when(t >= LAG)
                    def _():
                        xy_mid(squares, step, part, t - LAG)

            over_tiles(product_tile)

        over_tiles(lambda t: xy_mid(squares, step, last, t), tiles - LAG)
        xy_fin(squares, step, last, 0)

        def cubic_tile(t):
            @pl.when(t < tiles - 1)
            def _():
                xy_fin(squares, step, last, t + 1)

            for part in range(n_parts):
                xy_done(squares, step, part, t)
            cubic = jnp.dot(panel[...], squares[t], preferred_element_type=jnp.float32)
            for part in range(n_parts):
                xy_sent(squares, step, part, t)
            finish(t, cubic)

        over_tiles(cubic_tile)

    roots = []

    def first_scale():
        reduce_mid(0)
        total = reduce_end(0)
        scale = target * order / (jnp.sum(total[4:5, :], axis=1, keepdims=True) + 1e-06)
        roots.append(jnp.sqrt(scale))
        return scale

    def finish_first(t, cubic):
        wide = panel1[:, columns_of(z, t)].astype(jnp.float32)
        value = roots[0] * (1.5 * wide - 0.5 * cubic)
        current[t] = value
        rounded = value.astype(jnp.bfloat16)
        panel2[:, columns_of(z, t)] = rounded
        cols[t, rows_of(r), :] = rounded
        z_start(1, 0, t)
        xy_start(cols, 1, None, t)
        add_stats(0, t, value)

    def finish_second(t, cubic):
        value = 1.5 * current[t] - 0.5 * cubic
        out_ref[:, pl.ds(pl.multiple_of(t * TILE, TILE), TILE)] = value
        add_stats(2, t, value)

    step_of(0, first_scale, finish_first)
    step_of(1, lambda: None, finish_second)

    reduce_start(1, stats[...])
    reduce_mid(1)
    total = reduce_end(1)
    sums = jnp.sum(total, axis=1, keepdims=True)
    norms = jnp.sqrt(sums)
    trace_ref[0] = sums[0, 0]
    trace_ref[1] = sums[2, 0]
    frob_ref[0] = norms[1, 0]
    frob_ref[1] = norms[3, 0]

    def clear(t):
        for step in range(ITERS):
            for part in range(n_parts):
                z_sent(step, part, t)

    over_tiles(clear)


def in_one_kernel(n_row, n_col, matrix):
    rows, width = matrix.shape
    tiles = width // TILE
    order = rows * n_row
    n_parts = len(row_parts(rows))
    narrow = jnp.bfloat16
    return pl.pallas_call(
        functools.partial(kernel, n_row, n_col),
        out_shape=(
            pltpu.VMEM((rows, width), jnp.float32),
            jax.ShapeDtypeStruct((ITERS,), jnp.float32),
            jax.ShapeDtypeStruct((ITERS,), jnp.float32),
        ),
        in_specs=[pl.BlockSpec(memory_space=pl.ANY)],
        out_specs=(
            pl.BlockSpec(memory_space=pltpu.VMEM),
            pl.BlockSpec(memory_space=pltpu.SMEM),
            pl.BlockSpec(memory_space=pltpu.SMEM),
        ),
        scratch_shapes=[
            pltpu.VMEM((rows, width * n_col), narrow),
            pltpu.VMEM((rows, width * n_col), narrow),
            pltpu.VMEM((tiles, order, TILE), narrow),
            pltpu.VMEM((tiles, order, TILE), narrow),
            pltpu.VMEM((tiles, rows, TILE), jnp.float32),
            pltpu.VMEM((8, 128), jnp.float32),
            pltpu.VMEM((2, n_row, 8, 128), jnp.float32),
            pltpu.VMEM((2, n_col, 8, 128), jnp.float32),
            pltpu.SemaphoreType.DMA((ITERS * (n_parts + 1), tiles, KINDS)),
            pltpu.SemaphoreType.DMA((ITERS * (n_parts + 1), tiles, KINDS)),
            pltpu.SemaphoreType.DMA((ITERS * n_parts, tiles, 2 * (n_col - 1))),
            pltpu.SemaphoreType.DMA((ITERS * n_parts, tiles, 2 * (n_col - 1))),
            pltpu.SemaphoreType.DMA((2, n_row + n_col)),
            pltpu.SemaphoreType.DMA((2, n_row + n_col)),
            pltpu.SemaphoreType.DMA((tiles,)),
        ],
        compiler_params=pltpu.CompilerParams(
            collective_id=0, has_side_effects=True, vmem_limit_bytes=56 * 1024 * 1024
        ),
    )(matrix)


def solution(mesh):
    in_specs = (P("row", "col"),)
    out_specs = (P("row", "col"), P(), P())
    n_row, n_col = mesh.shape["row"], mesh.shape["col"]

    def body(matrix):
        square_plane = n_row == 2 * 2 * 2 and n_col == 2 * 2
        if square_plane and matrix.shape[1] % TILE == 0 and matrix.shape[0] % (5 * 16) == 0:
            return in_one_kernel(n_row, n_col, matrix)
        return on_device(matrix)

    return jax.shard_map(
        body, mesh=mesh, in_specs=in_specs, out_specs=out_specs, check_vma=False
    )
```
